32 devices in a mesh: conf: 2 (over y), row: 4 (over z), col: 4 (over x, core).
Axes of the slice: x: 2, y: 2, z: 4, core: 2. Of those that a mesh axis runs over, the one named last changes fastest.
Arguments:
- pair_state: bfloat16 [512, 256, 128], P(('conf', 'row'), 'col'), parts along dimension 0, may hold values from -6 to 6
- token_kinds: int32 [512], P('conf'), parts along dimension 0, may hold values from 0 to 31
- first_type_table: bfloat16 [32, 128], replicated, may hold values from -3 to 3
- second_type_table: bfloat16 [32, 128], replicated, may hold values from -3 to 3
- alignment_state: bfloat16 [64, 16384], P(None, ('conf', 'row', 'col')), parts along dimension 1, may hold values from -6 to 6
- alignment_index: int32 [64, 512], P(None, ('conf', 'row', 'col')), parts along dimension 1, may hold values from 0 to 31
- alignment_table: bfloat16 [32, 32], replicated, may hold values from -3 to 3
- first_weight: bfloat16 [32, 32], replicated, may hold values from -1 to 1
- second_weight: bfloat16 [32, 32], replicated, may hold values from -1 to 1
- outer_product_weight: bfloat16 [1024, 128], replicated, may hold values from -1.5 to 1.5
- outer_product_bias: bfloat16 [128], replicated, may hold values from -4 to 4
- pair_block_mask: int32 [32, 16], P(('conf', 'row'), 'col'), parts along dimension 0, may hold values 0 or 1
- transition_gain: float32 [128], replicated, may hold values from 0.25 to 1.75
- transition_gate_up: bfloat16 [128, 1024], replicated, may hold values from -0.5 to 0.5
- transition_down: bfloat16 [512, 128], replicated, may hold values from -0.25 to 0.25
- distance_weight: bfloat16 [128, 64], replicated, may hold values from -0.5 to 0.5
- distance_bias: float32 [64], replicated, may hold values from -4 to 4
Outputs:
- pair_out: bfloat16 [512, 256, 128], P(('conf', 'row'), 'col'), parts along dimension 0
- distogram: bfloat16 [512, 16384], P(('conf', 'row'), 'col'), parts along dimension 0
The draws below stay inside these ranges and needn't reach their ends.
There are 2 independent parts, one for each index of `conf`. The reference program is written for one: setup_inputs(seed, part) draws one part's arguments, and reference() takes and returns one part's arrays. A program takes and returns all parts, laid end to end along the dimension named above; an argument that names none is the same for every part. Nothing has to cross between parts.
All inputs are finite; a program needn't handle non-finite values. No bound on the sum of `pair_block_mask` on one device may be relied on, other than what follows from the above.
Results may differ from the reference program's by a relative error of at most 0.0071.
Values may be sent and summed in bfloat16 or wider, within the bound.
A program may use at most 64 MiB of HBM per device.

```python
import jax
import jax.numpy as jnp
from jax import lax

TOKEN_COUNT = 256
ALIGN_ROWS = 64
ALIGN_FEATURES = 32
C = 32
CZ = 128
HID = 512
BINS = 64
RESIDUE_KINDS = 32
MB = 16


def touch_ends(drawn, rng, least, top_value):
    longest = drawn.shape.index(max(drawn.shape))
    spots = []
    for shift in (0, 1):
        where = [jax.random.randint(jax.random.fold_in(rng, axis), (), 0, length) for axis, length in enumerate(drawn.shape)]
        where[longest] = (where[longest] + shift) % drawn.shape[longest]
        spots.append(tuple(where))
    return drawn.at[spots[0]].set(least).at[spots[1]].set(top_value)


def level_of(rng, extent, shards, smallest, top_value):
    loudness = 1.0
    for dim, parts in shards:
        draws = jax.random.uniform(jax.random.fold_in(jax.random.fold_in(rng, 6), dim), (parts,), jnp.float32, smallest / len(shards), top_value / len(shards))
        loudness = loudness * jnp.repeat(jnp.exp(draws), extent[dim] // parts).reshape((-1,) + (1,) * (len(extent) - 1 - dim))
    return loudness


def normal_values(rng, extent, scale, most, pieces=(), kind=jnp.bfloat16):
    array = jax.random.normal(rng, extent, jnp.float32) * scale
    if len(pieces) > 0:
        array = level_of(rng, extent, pieces, -0.22, 0.18) * array
    return jnp.clip(array, min=-most, max=most).astype(kind)


def setup_inputs(seed: int = 0, part: int = 0) -> dict:
    keys = jax.random.split(jax.random.key(seed), 18)
    own_keys = jax.random.split(jax.random.fold_in(keys[17], part), 18)
    return {
        "pair_state": normal_values(own_keys[0], (TOKEN_COUNT, TOKEN_COUNT, CZ), 1.0, 6.0, ((0, 4), (1, 4))),
        "token_kinds": touch_ends(jax.random.randint(own_keys[1], (TOKEN_COUNT,), 0, RESIDUE_KINDS), jax.random.fold_in(own_keys[1], 1), 0, RESIDUE_KINDS - 1).astype(jnp.int32),
        "first_type_table": normal_values(keys[2], (RESIDUE_KINDS, CZ), 0.5, 3.0),
        "second_type_table": normal_values(keys[3], (RESIDUE_KINDS, CZ), 0.5, 3.0),
        "alignment_state": normal_values(own_keys[4], (ALIGN_ROWS, TOKEN_COUNT * ALIGN_FEATURES), 1.0, 6.0, ((1, 16),)),
        "alignment_index": touch_ends(jax.random.randint(own_keys[5], (ALIGN_ROWS, TOKEN_COUNT), 0, RESIDUE_KINDS), jax.random.fold_in(own_keys[5], 1), 0, RESIDUE_KINDS - 1).astype(jnp.int32),
        "alignment_table": normal_values(keys[6], (RESIDUE_KINDS, ALIGN_FEATURES), 0.5, 3.0),
        "first_weight": normal_values(keys[7], (ALIGN_FEATURES, C), ALIGN_FEATURES ** -0.5, 1.0),
        "second_weight": normal_values(keys[8], (ALIGN_FEATURES, C), ALIGN_FEATURES ** -0.5, 1.0),
        "outer_product_weight": normal_values(keys[9], (C * C, CZ), (C * C // 64) ** -0.5, 1.5),
        "outer_product_bias": normal_values(keys[10], (CZ,), 1.0, 4.0),
        "pair_block_mask": touch_ends((jax.random.randint(own_keys[11], (TOKEN_COUNT // MB, TOKEN_COUNT // MB), 0, 4) < 3).astype(jnp.int32), jax.random.fold_in(own_keys[11], 1), 0, 1),
        "transition_gain": jnp.clip(1.0 + 0.15 * jax.random.normal(keys[12], (CZ,), jnp.float32), 0.25, 1.75),
        "transition_gate_up": normal_values(keys[13], (CZ, 2 * HID), CZ ** -0.5, 0.5),
        "transition_down": normal_values(keys[14], (HID, CZ), HID ** -0.5, 0.25),
        "distance_weight": normal_values(keys[15], (CZ, BINS), CZ ** -0.5, 0.5),
        "distance_bias": normal_values(keys[16], (BINS,), 1.0, 4.0, (), jnp.float32),
    }


EPSILON = 1e-05

def reference(pair_state, token_kinds, first_type_table, second_type_table, alignment_state, alignment_index, alignment_table, first_weight, second_weight, outer_product_weight, outer_product_bias, pair_block_mask, transition_gain, transition_gate_up, transition_down, distance_weight, distance_bias):
    embedded_input = (alignment_state.reshape(ALIGN_ROWS, TOKEN_COUNT, ALIGN_FEATURES).astype(jnp.float32) + alignment_table[alignment_index].astype(jnp.float32)).astype(jnp.bfloat16)
    left_proj = jnp.einsum('snm,mc->snc', embedded_input.astype(jnp.float32), first_weight.astype(jnp.float32)).astype(jnp.bfloat16)
    right_proj = jnp.einsum('snm,mc->snc', embedded_input.astype(jnp.float32), second_weight.astype(jnp.float32)).astype(jnp.bfloat16)
    right_float = right_proj.astype(jnp.float32)
    left_embed = first_type_table[token_kinds].astype(jnp.float32)
    right_embed = second_type_table[token_kinds].astype(jnp.float32)
    mask_full = jnp.repeat(jnp.repeat(pair_block_mask, MB, axis=0), MB, axis=1).astype(jnp.float32)
    block_rows = 16
    dist_float = distance_weight.astype(jnp.float32)

    def one_block(block_index):
        first_row = block_index * block_rows
        left_part = lax.dynamic_slice_in_dim(left_proj, first_row, block_rows, 1).astype(jnp.float32)
        outer_average = jnp.einsum('sic,sje->ijce', left_part, right_float) / ALIGN_ROWS
        outer_average = outer_average.astype(jnp.bfloat16).reshape(block_rows * TOKEN_COUNT, C * C)
        update = jnp.dot(outer_average, outer_product_weight, preferred_element_type=jnp.float32).reshape(block_rows, TOKEN_COUNT, CZ)
        update = update + outer_product_bias.astype(jnp.float32)
        pair_part = lax.dynamic_slice_in_dim(pair_state, first_row, block_rows, 0).astype(jnp.float32)
        embed_part = lax.dynamic_slice_in_dim(left_embed, first_row, block_rows, 0)
        mask_part = lax.dynamic_slice_in_dim(mask_full, first_row, block_rows, 0)
        start_pair = pair_part + embed_part[:, None, :] + right_embed[None, :, :] + mask_part[:, :, None] * update
        chan_mean = lax.optimization_barrier(jnp.mean(start_pair, axis=-1, keepdims=True))
        centered = start_pair - chan_mean
        chan_var = lax.optimization_barrier(jnp.mean(centered * centered, axis=-1, keepdims=True))
        normed = (centered * lax.rsqrt(chan_var + EPSILON) * transition_gain).astype(jnp.bfloat16)
        gate_up = jnp.dot(normed.reshape(block_rows * TOKEN_COUNT, CZ), transition_gate_up, preferred_element_type=jnp.float32)
        hidden = (jax.nn.silu(gate_up[:, :HID]) * gate_up[:, HID:]).astype(jnp.bfloat16)
        result = (start_pair + jnp.dot(hidden, transition_down, preferred_element_type=jnp.float32).reshape(block_rows, TOKEN_COUNT, CZ)).astype(jnp.bfloat16)
        part = jnp.einsum('ijc,cb->ijb', result.astype(jnp.float32), dist_float).astype(jnp.bfloat16)
        return (result, part)
    pair_out, dist_part = lax.map(one_block, jnp.arange(TOKEN_COUNT // block_rows, dtype=jnp.int32))
    pair_out = pair_out.reshape(TOKEN_COUNT, TOKEN_COUNT, CZ)
    dist_part = dist_part.reshape(TOKEN_COUNT, TOKEN_COUNT, BINS)

    def dist_block(block_index):
        first_row = block_index * block_rows
        direct = lax.dynamic_slice_in_dim(dist_part, first_row, block_rows, 0).astype(jnp.float32)
        mirrored = jnp.swapaxes(lax.dynamic_slice_in_dim(dist_part, first_row, block_rows, 1), 0, 1).astype(jnp.float32)
        return (direct + mirrored + distance_bias).astype(jnp.bfloat16)
    distogram = lax.map(dist_block, jnp.arange(TOKEN_COUNT // block_rows, dtype=jnp.int32)).reshape(TOKEN_COUNT, TOKEN_COUNT * BINS)
    return (pair_out, distogram)
```

```python
import functools

import jax
import jax.numpy as jnp
from jax import lax
from jax.experimental import pallas as pl
from jax.experimental.pallas import tpu as pltpu
from jax.sharding import PartitionSpec as P

EPSILON = 1e-05
LANES = 128
MESH = pl.DeviceIdType.MESH


def project_tokens(
    depth, state_ref, index_ref, table_ref, first_weight_ref, second_weight_ref, left_ref, right_ref
):
    levels, features = table_ref.shape
    width = first_weight_ref.shape[1]
    tokens = index_ref.shape[0]
    per_tile = LANES // features
    tiles = tokens // per_tile
    packed = LANES // depth

    def iota(shape, axis):
        return lax.broadcasted_iota(jnp.int32, shape, axis)

    def indicator(inside):
        return inside.astype(jnp.float32).astype(jnp.bfloat16)

    def dot(left, right, dims):
        return lax.dot_general(left, right, (dims, ((), ())), preferred_element_type=jnp.float32)

    repeat = indicator(iota((LANES, features), 0) % features == iota((LANES, features), 1))
    wide = per_tile * levels
    repeat_levels = indicator(iota((wide, levels), 0) % levels == iota((wide, levels), 1))
    table_rows = dot(repeat_levels, table_ref[...], ((1,), (0,))).astype(jnp.bfloat16)
    table_wide = jnp.where(
        iota((wide, LANES), 0) // levels == iota((wide, LANES), 1) // features,
        dot(table_rows, repeat, ((1,), (1,))),
        0.0,
    ).astype(jnp.bfloat16)
    first_wide = dot(first_weight_ref[...], repeat, ((0,), (1,))).astype(jnp.bfloat16)
    second_wide = dot(second_weight_ref[...], repeat, ((0,), (1,))).astype(jnp.bfloat16)

    rows = width // packed * tokens
    token_of = iota((rows, LANES), 0) % tokens
    slot_of = iota((rows, LANES), 1) // features
    picks = []
    for position in range(packed):
        pick = indicator(
            iota((rows, width), 0) // tokens * packed + position == iota((rows, width), 1)
        )
        spread = dot(pick, second_wide, ((1,), (0,)))
        for tile in range(tiles):
            picks.append(
                jnp.where(token_of == tile * per_tile + slot_of, spread, 0.0).astype(jnp.bfloat16)
            )

    spread_index = indicator(
        iota((tokens, tokens * levels), 1) // levels == iota((tokens, tokens * levels), 0)
    )
    index_wide = dot(
        index_ref[...].astype(jnp.float32).astype(jnp.bfloat16), spread_index, ((0,), (0,))
    )
    level_of = (iota((depth, tokens * levels), 1) % levels).astype(jnp.float32)
    onehot = indicator(index_wide == level_of)
    lane_slot = iota((depth, LANES), 1) // features
    embedded = []
    for tile in range(tiles):
        looked = dot(onehot[:, tile * wide : (tile + 1) * wide], table_wide, ((1,), (0,)))
        state = state_ref[:, tile * LANES : (tile + 1) * LANES].astype(jnp.float32)
        value = (state + looked).astype(jnp.bfloat16).astype(jnp.float32)
        embedded.append(value.astype(jnp.bfloat16))
        stack = jnp.concatenate(
            [
                jnp.where(lane_slot == slot, value, 0.0).astype(jnp.bfloat16)
                for slot in range(per_tile)
            ],
            axis=0,
        )
        left_ref[tile] = dot(first_wide, stack, ((1,), (1,))).astype(jnp.bfloat16)

    blank = jnp.zeros((depth, LANES), jnp.bfloat16)
    parts = []
    for position in range(packed):
        for tile in range(tiles):
            parts.append(
                jnp.concatenate(
                    [embedded[tile] if place == position else blank for place in range(packed)], axis=0
                )
            )
    right = dot(
        jnp.concatenate(picks, axis=1), jnp.concatenate(parts, axis=1), ((1,), (1,))
    )
    for place in range(width // packed):
        right_ref[:, place * LANES : (place + 1) * LANES] = right[
            place * tokens : (place + 1) * tokens
        ].astype(jnp.bfloat16)


def kernel(
    ranks,
    depth,
    chunks,
    pair_hbm,
    kinds_hbm,
    first_table_hbm,
    second_table_hbm,
    state_hbm,
    index_hbm,
    align_table_hbm,
    first_weight_hbm,
    second_weight_hbm,
    outer_weight_hbm,
    outer_bias_hbm,
    mask_hbm,
    gain_hbm,
    gate_up_hbm,
    down_hbm,
    weight_hbm,
    dist_bias_hbm,
    pair_out_ref,
    dist_out_ref,
    left_ref,
    right_ref,
    left_all,
    right_all,
    outer_ref,
    outer_weight_raw,
    outer_weight_float,
    outer_weight_ref,
    pair_float,
    right_embed_ref,
    left_embed_ref,
    mirror_send,
    mirror_recv,
    own_part,
    start_ref,
    normed_ref,
    left_send_sem,
    left_recv_sem,
    right_send_sem,
    right_recv_sem,
    mirror_send_sem,
    mirror_recv_sem,
    relay_recv,
    relay_recv_sem,
    forward_send_sem,
    dist_weight_wide,
    dist_bias_wide,
    embed_all,
    pair_ref,
    kinds_ref,
    first_table_ref,
    second_table_ref,
    state_ref,
    index_ref,
    align_table_ref,
    first_weight_ref,
    second_weight_ref,
    outer_bias_ref,
    mask_ref,
    gain_ref,
    gate_up_ref,
    down_ref,
    weight_ref,
    dist_bias_ref,
    load_sem,
):
    conf = lax.axis_index("conf")
    row = lax.axis_index("row")
    col = lax.axis_index("col")
    local_groups, width, span = left_ref.shape
    local_tokens = right_ref.shape[0]
    block = pair_ref.shape[0]
    groups = left_all.shape[0]
    members = span // depth
    pairs = members * block
    hid = down_ref.shape[0]
    pitch = pair_float.shape[0] // block
    diagonal = row == col

    def load(place, source, target):
        return pltpu.make_async_copy(source, target, load_sem.at[place])

    early = [
        load(0, index_hbm, index_ref),
        load(1, state_hbm, state_ref),
        load(2, align_table_hbm, align_table_ref),
        load(3, first_weight_hbm, first_weight_ref),
        load(4, second_weight_hbm, second_weight_ref),
    ]
    later = [
        load(5, kinds_hbm, kinds_ref),
        load(6, first_table_hbm, first_table_ref),
        load(7, second_table_hbm, second_table_ref),
        load(8, weight_hbm, weight_ref),
        load(9, dist_bias_hbm, dist_bias_ref),
        load(10, outer_weight_hbm, outer_weight_raw),
    ]
    last_loads = [
        load(11, pair_hbm, pair_ref),
        load(12, outer_bias_hbm, outer_bias_ref),
        load(13, mask_hbm, mask_ref),
        load(14, gain_hbm, gain_ref),
        load(15, gate_up_hbm, gate_up_ref),
        load(16, down_hbm, down_ref),
    ]
    for copy in early:
        copy.start()

    barrier = pltpu.get_barrier_semaphore()
    for step in range(1, ranks):
        pl.semaphore_signal(
            barrier, inc=1, device_id=(conf, row, lax.rem(col + step, ranks)), device_id_type=MESH
        )
    for step in range(ranks):
        source = lax.rem(col + step, ranks)

        @pl.when(jnp.logical_or(jnp.logical_not(diagonal), source != col))
        def _():
            pl.semaphore_signal(
                barrier, inc=1, device_id=(conf, col, source), device_id_type=MESH
            )

    @pl.when(jnp.logical_not(diagonal))
    def _():
        pl.semaphore_signal(barrier, inc=1, device_id=(conf, col, row), device_id_type=MESH)

    for copy in later + last_loads:
        copy.start()
    for copy in early:
        copy.wait()
    project_tokens(
        depth, state_ref, index_ref, align_table_ref, first_weight_ref, second_weight_ref, left_ref, right_ref
    )

    @pl.when(jnp.logical_not(diagonal))
    def _():
        pl.semaphore_wait(barrier, 2 * ranks)

    @pl.when(diagonal)
    def _():
        pl.semaphore_wait(barrier, 2 * (ranks - 1))

    def left_copy(peer, slot):
        return pltpu.make_async_remote_copy(
            src_ref=left_ref,
            dst_ref=left_all.at[pl.ds(slot * local_groups, local_groups)],
            send_sem=left_send_sem.at[peer],
            recv_sem=left_recv_sem.at[slot],
            device_id=(conf, row, peer),
            device_id_type=MESH,
        )

    def right_copy(target, slot):
        return pltpu.make_async_remote_copy(
            src_ref=right_ref,
            dst_ref=right_all.at[slot],
            send_sem=right_send_sem.at[target],
            recv_sem=right_recv_sem.at[slot],
            device_id=(conf, target, row),
            device_id_type=MESH,
        )

    for step in range(ranks):
        target = lax.rem(row + step, ranks)

        @pl.when(jnp.logical_or(jnp.logical_not(diagonal), target != row))
        def _():
            right_copy(target, col).start()

    for step in range(1, ranks):
        left_copy(lax.rem(col + step, ranks), col).start()

    left_all[pl.ds(col * local_groups, local_groups)] = left_ref[...]

    @pl.when(diagonal)
    def _():
        right_all[col] = right_ref[...]

    for copy in later:
        copy.wait()
    tokens = kinds_ref.shape[1]
    levels = lax.broadcasted_iota(jnp.int32, (first_table_ref.shape[0], tokens), 0)
    onehot = (levels == kinds_ref[...]).astype(jnp.float32).astype(jnp.bfloat16)
    for table_ref, embed_ref, place in (
        (first_table_ref, left_embed_ref, row),
        (second_table_ref, right_embed_ref, col),
    ):
        embed_all[...] = lax.dot_general(
            onehot, table_ref[...], (((0,), (0,)), ((), ())), preferred_element_type=jnp.float32
        )
        embed_ref[...] = embed_all[pl.ds(pl.multiple_of(place * block, block), block), :]
    bins = dist_bias_ref.shape[1]
    for place in range(2):
        dist_bias_wide[:, place * bins : (place + 1) * bins] = dist_bias_ref[...]
    dist_weight_wide[...] = jnp.zeros_like(dist_weight_wide)
    depth_of = weight_ref.shape[1]
    for place in range(2):
        dist_weight_wide[
            place * bins : (place + 1) * bins, place * depth_of : (place + 1) * depth_of
        ] = weight_ref[...]

    outer_weight_float[...] = outer_weight_raw[...].astype(jnp.float32)
    for index in range(width):
        outer_weight_ref[index * width : (index + 1) * width, :] = outer_weight_float[
            pl.ds(index, width, stride=width), :
        ].astype(jnp.bfloat16)
    for copy in last_loads:
        copy.wait()

    for step in range(1, ranks):
        peer = lax.rem(col + step, ranks)
        left_copy(peer, peer).wait_recv()
    for step in range(ranks):
        source = lax.rem(col + step, ranks)

        @pl.when(jnp.logical_or(jnp.logical_not(diagonal), source != col))
        def _():
            right_copy(source, source).wait_recv()

    lane = lax.broadcasted_iota(jnp.int32, (width, LANES), 1)
    packed = LANES // depth
    span_tiles = span // LANES
    zero = jnp.zeros((width, LANES), jnp.bfloat16)
    spans = right_ref.shape[1] // span

    def right_rows(place):
        found = [
            right_all[source, :, place * span : (place + 1) * span] for source in range(ranks)
        ]
        if local_tokens % 16 == 0:
            return jnp.concatenate(found, axis=0)
        return jnp.concatenate([part.astype(jnp.float32) for part in found], axis=0).astype(jnp.bfloat16)

    def outer(group):
        found = [
            left_all[group, :, tile * LANES : (tile + 1) * LANES].astype(jnp.float32)
            for tile in range(span_tiles)
        ]
        spread = []
        for member in range(members):
            kept = []
            for position in range(packed):
                shift = (position - member % packed) * depth % LANES
                moved = found[member // packed]
                moved = moved if shift == 0 else pltpu.roll(moved, shift, 1)
                inside = jnp.logical_and(lane >= position * depth, lane < (position + 1) * depth)
                kept.append(jnp.where(inside, moved, 0.0).astype(jnp.bfloat16))
            for place in range(members):
                spread.append(
                    jnp.concatenate(
                        [kept[place % packed] if t == place // packed else zero for t in range(span_tiles)],
                        axis=1,
                    )
                )
        rows = jnp.concatenate([right_rows(place) for place in range(spans)], axis=0)
        wide = members * width
        for first in range(0, members, 2):
            product = lax.dot_general(
                rows,
                jnp.concatenate(spread[first * members : (first + 2) * members], axis=0),
                (((1,), (1,)), ((), ())),
                preferred_element_type=jnp.float32,
            ).astype(jnp.bfloat16)
            for member in range(2):
                for place in range(spans):
                    outer_ref[
                        (first + member) * block : (first + member + 1) * block,
                        place * wide : (place + 1) * wide,
                    ] = product[
                        place * block : (place + 1) * block, member * wide : (member + 1) * wide
                    ]

    chips = ranks // 2
    far = (col // 2 == lax.rem(row // 2 + chips // 2, chips)) if chips > 1 else None
    relay = (col // 2 == row // 2) if chips > 1 else None
    relay_col = row // 2 * 2 + lax.rem(col, 2)
    served_col = lax.rem(row // 2 + chips // 2, max(chips, 1)) * 2 + lax.rem(col, 2)
    part_tiles = block // 4 // chunks

    def half_of(chunk, half):
        return pl.ds((chunk * 2 + half) * part_tiles, part_tiles)

    def mirror_copy(chunk, half):
        return pltpu.make_async_remote_copy(
            src_ref=mirror_send.at[half_of(chunk, half)],
            dst_ref=mirror_recv.at[half_of(chunk, half)],
            send_sem=mirror_send_sem.at[half, chunk],
            recv_sem=mirror_recv_sem.at[half, chunk],
            device_id=(conf, col, row),
            device_id_type=MESH,
        )

    def relay_copy(chunk, target):
        return pltpu.make_async_remote_copy(
            src_ref=mirror_send.at[half_of(chunk, 1)],
            dst_ref=relay_recv.at[chunk],
            send_sem=mirror_send_sem.at[1, chunk],
            recv_sem=relay_recv_sem.at[chunk],
            device_id=(conf, row, target),
            device_id_type=MESH,
        )

    def forward_copy(chunk):
        return pltpu.make_async_remote_copy(
            src_ref=relay_recv.at[chunk],
            dst_ref=mirror_recv.at[half_of(chunk, 1)],
            send_sem=forward_send_sem.at[chunk],
            recv_sem=mirror_recv_sem.at[1, chunk],
            device_id=(conf, served_col, row),
            device_id_type=MESH,
        )

    def send_chunk(chunk):
        @pl.when(jnp.logical_not(diagonal))
        def _():
            mirror_copy(chunk, 0).start()

        if chips > 1:

            @pl.when(far)
            def _():
                relay_copy(chunk, relay_col).start()

            @pl.when(jnp.logical_not(jnp.logical_or(diagonal, far)))
            def _():
                mirror_copy(chunk, 1).start()
        else:

            @pl.when(jnp.logical_not(diagonal))
            def _():
                mirror_copy(chunk, 1).start()

    def pass_on(chunk):
        relay_copy(chunk, served_col).wait_recv()
        forward_copy(chunk).start()

    mask_rows, mask_cols = mask_ref.shape
    groups_per_mask = groups // mask_rows
    mask_side = block // mask_cols
    tiles = block // 2 // chunks
    channels = pair_ref.shape[2]

    def project():
        return jnp.dot(outer_ref[...], outer_weight_ref[...], preferred_element_type=jnp.float32)

    def normalise(group, summed):
        update = summed * (1.0 / depth) + outer_bias_ref[...].astype(jnp.float32)
        mask_col = jnp.concatenate(
            [
                jnp.full(
                    (mask_side, channels),
                    mask_ref[group // groups_per_mask, place].astype(jnp.float32),
                    jnp.float32,
                )
                for place in range(mask_cols)
            ],
            axis=0,
        )
        first = pl.multiple_of(group * members, members)
        state = pair_ref[pl.ds(first, members)].astype(jnp.float32)
        left_embed = left_embed_ref[pl.ds(first, members), :]
        start = (
            state
            + left_embed[:, None, :]
            + right_embed_ref[...][None]
            + mask_col[None] * update.reshape(members, block, channels)
        ).reshape(pairs, channels)
        mean = jnp.mean(start, axis=-1, keepdims=True)
        centered = start - mean
        variance = jnp.mean(centered * centered, axis=-1, keepdims=True)
        normed = (centered * lax.rsqrt(variance + EPSILON) * gain_ref[...]).astype(jnp.bfloat16)
        return start, normed

    def expand(normed):
        hidden = []
        for place in range(0, hid, LANES):
            weight = jnp.concatenate(
                [
                    gate_up_ref[:, place : place + LANES],
                    gate_up_ref[:, hid + place : hid + place + LANES],
                ],
                axis=1,
            )
            gate_up = jnp.dot(normed, weight, preferred_element_type=jnp.float32)
            half = 0.5 * gate_up[:, :LANES]
            hidden.append(((half + half * jnp.tanh(half)) * gate_up[:, LANES:]).astype(jnp.bfloat16))
        return jnp.concatenate(hidden, axis=1)

    def contract(start, hidden):
        branch = jnp.dot(hidden, down_ref[...], preferred_element_type=jnp.float32)
        result = (start + branch).astype(jnp.bfloat16)
        shaped = result.reshape(members // 2, 2, block, channels)
        joined = jnp.concatenate([shaped[:, 0], shaped[:, 1]], axis=-1).reshape(
            members // 2 * block, 2 * channels
        )
        part = lax.dot_general(
            joined, dist_weight_wide[...], (((1,), (1,)), ((), ())),
            preferred_element_type=jnp.float32,
        )
        return result, part.astype(jnp.bfloat16).reshape(members // 2, block, LANES)

    last = groups - 1
    outer(0)
    start_ref[...], normed_ref[...] = normalise(0, project())
    outer(1)

    def group_step(group, carry):
        start = start_ref[...]
        hidden = expand(normed_ref[...])
        summed = project()
        result, part = contract(start, hidden)
        next_start, next_normed = normalise(jnp.minimum(group + 1, last), summed)
        outer(jnp.minimum(group + 2, last))
        first = pl.multiple_of(group * members, members)
        pair_out_ref[pl.ds(first, members)] = result.reshape(members, block, channels)
        wide = result.astype(jnp.float32)
        for member in range(members):
            pair_float[pl.ds((first + member) * pitch, block), :] = wide[
                member * block : (member + 1) * block
            ]
        mirror_send[pl.ds(group * (members // 2), members // 2)] = part
        start_ref[...] = next_start
        normed_ref[...] = next_normed
        return carry

    groups_per_chunk = groups // chunks

    def chunk_step(chunk, carry):
        lax.fori_loop(chunk * groups_per_chunk, (chunk + 1) * groups_per_chunk, group_step, 0)

        send_chunk(chunk)
        if chips > 1:

            @pl.when(jnp.logical_and(relay, chunk > 0))
            def _():
                pass_on(chunk - 1)

        return carry

    lax.fori_loop(0, chunks, chunk_step, 0)

    if chips > 1:

        @pl.when(relay)
        def _():
            pass_on(chunks - 1)

    def own_step(tile, carry):
        even = pair_float[pl.ds(2 * tile, block, stride=pitch), :]
        odd = pair_float[pl.ds(2 * tile + 1, block, stride=pitch), :]
        joined = jnp.concatenate([even, odd], axis=1).astype(jnp.bfloat16)
        part = lax.dot_general(
            joined, dist_weight_wide[...], (((1,), (1,)), ((), ())),
            preferred_element_type=jnp.float32,
        )
        own_part[tile] = part.astype(jnp.bfloat16).astype(jnp.float32) + dist_bias_wide[...]
        return carry

    lax.fori_loop(0, block // 2, own_step, 0, unroll=4)

    def finish(tiles_from):
        def step(chunk, carry):
            @pl.when(jnp.logical_not(diagonal))
            def _():
                mirror_copy(chunk, 0).wait_recv()
                mirror_copy(chunk, 1).wait_recv()

            for tile in range(tiles):
                index = chunk * tiles + tile
                total = own_part[index] + tiles_from[index].astype(jnp.float32)
                dist_out_ref[:, pl.ds(pl.multiple_of(index * LANES, LANES), LANES)] = total.astype(
                    jnp.bfloat16
                )
            return carry

        lax.fori_loop(0, chunks, step, 0)

    @pl.when(diagonal)
    def _():
        finish(mirror_send)

    @pl.when(jnp.logical_not(diagonal))
    def _():
        finish(mirror_recv)
        for chunk in range(chunks):
            mirror_copy(chunk, 0).wait_send()
            mirror_copy(chunk, 1).wait_send()

    if chips > 1:

        @pl.when(relay)
        def _():
            for chunk in range(chunks):
                forward_copy(chunk).wait_send()

    for step in range(ranks):
        target = lax.rem(row + step, ranks)

        @pl.when(jnp.logical_or(jnp.logical_not(diagonal), target != row))
        def _():
            right_copy(target, col).wait_send()

    for step in range(1, ranks):
        left_copy(lax.rem(col + step, ranks), col).wait_send()


def local(
    ranks,
    pair_state,
    token_kinds,
    first_type_table,
    second_type_table,
    alignment_state,
    alignment_index,
    alignment_table,
    first_weight,
    second_weight,
    outer_product_weight,
    outer_product_bias,
    pair_block_mask,
    transition_gain,
    transition_gate_up,
    transition_down,
    distance_weight,
    distance_bias,
):
    block = pair_state.shape[0]
    channels = pair_state.shape[2]
    depth, local_tokens = alignment_index.shape
    features = alignment_state.shape[1] // local_tokens
    width = first_weight.shape[1]
    bins = distance_weight.shape[1]
    members = 2 * LANES // depth
    groups = block // members
    local_groups = local_tokens // members
    chunks = block // 8

    vmem = pl.BlockSpec(memory_space=pltpu.VMEM)
    hbm = pl.BlockSpec(memory_space=pltpu.HBM)
    pair_out, distogram = pl.pallas_call(
        functools.partial(kernel, ranks, depth, chunks),
        out_shape=(
            jax.ShapeDtypeStruct(pair_state.shape, jnp.bfloat16),
            jax.ShapeDtypeStruct((block, block * bins), jnp.bfloat16),
        ),
        in_specs=[hbm] * 17,
        out_specs=(vmem, vmem),
        scratch_shapes=[
            pltpu.VMEM((local_groups, width, members * depth), jnp.bfloat16),
            pltpu.VMEM((local_tokens, width * depth), jnp.bfloat16),
            pltpu.VMEM((groups, width, members * depth), jnp.bfloat16),
            pltpu.VMEM((ranks, local_tokens, width * depth), jnp.bfloat16),
            pltpu.VMEM((members * block, width * width), jnp.bfloat16),
            pltpu.VMEM(outer_product_weight.shape, jnp.bfloat16),
            pltpu.VMEM(outer_product_weight.shape, jnp.float32),
            pltpu.VMEM(outer_product_weight.shape, jnp.bfloat16),
            pltpu.VMEM((block * (block + 1), channels), jnp.float32),
            pltpu.VMEM((block, channels), jnp.float32),
            pltpu.VMEM((block, channels), jnp.float32),
            pltpu.VMEM((block // 2, block, 2 * bins), jnp.bfloat16),
            pltpu.VMEM((block // 2, block, 2 * bins), jnp.bfloat16),
            pltpu.VMEM((block // 2, block, 2 * bins), jnp.float32),
            pltpu.VMEM((members * block, channels), jnp.float32),
            pltpu.VMEM((members * block, channels), jnp.bfloat16),
            pltpu.SemaphoreType.DMA((ranks,)),
            pltpu.SemaphoreType.DMA((ranks,)),
            pltpu.SemaphoreType.DMA((ranks,)),
            pltpu.SemaphoreType.DMA((ranks,)),
            pltpu.SemaphoreType.DMA((2, chunks)),
            pltpu.SemaphoreType.DMA((2, chunks)),
            pltpu.VMEM((chunks, block // 4 // chunks, block, 2 * bins), jnp.bfloat16),
            pltpu.SemaphoreType.DMA((chunks,)),
            pltpu.SemaphoreType.DMA((chunks,)),
            pltpu.VMEM((2 * bins, 2 * channels), jnp.bfloat16),
            pltpu.VMEM((1, 2 * bins), jnp.float32),
            pltpu.VMEM((token_kinds.shape[0], channels), jnp.float32),
            pltpu.VMEM(pair_state.shape, pair_state.dtype),
            pltpu.VMEM((1, token_kinds.shape[0]), jnp.int32),
            pltpu.VMEM(first_type_table.shape, jnp.bfloat16),
            pltpu.VMEM(second_type_table.shape, jnp.bfloat16),
            pltpu.VMEM(alignment_state.shape, jnp.bfloat16),
            pltpu.VMEM((local_tokens, depth), jnp.int32),
            pltpu.VMEM(alignment_table.shape, jnp.bfloat16),
            pltpu.VMEM(first_weight.shape, jnp.bfloat16),
            pltpu.VMEM(second_weight.shape, jnp.bfloat16),
            pltpu.VMEM((1, channels), jnp.bfloat16),
            pltpu.SMEM(pair_block_mask.shape, jnp.int32),
            pltpu.VMEM((1, channels), jnp.float32),
            pltpu.VMEM(transition_gate_up.shape, transition_gate_up.dtype),
            pltpu.VMEM(transition_down.shape, transition_down.dtype),
            pltpu.VMEM((bins, channels), jnp.bfloat16),
            pltpu.VMEM((1, bins), jnp.float32),
            pltpu.SemaphoreType.DMA((17,)),
        ],
        compiler_params=pltpu.CompilerParams(
            collective_id=0, has_side_effects=True, vmem_limit_bytes=60 * 1024 * 1024
        ),
    )(
        pair_state,
        token_kinds[None],
        first_type_table,
        second_type_table,
        alignment_state,
        alignment_index.T,
        alignment_table,
        first_weight,
        second_weight,
        outer_product_weight,
        outer_product_bias[None],
        pair_block_mask,
        transition_gain[None],
        transition_gate_up,
        transition_down,
        distance_weight.T,
        distance_bias[None],
    )
    return pair_out, distogram


def solution(mesh):
    in_specs = (
        P(("conf", "row"), "col", None),
        P("conf"),
        P(),
        P(),
        P(None, ("conf", "row", "col")),
        P(None, ("conf", "row", "col")),
        P(),
        P(),
        P(),
        P(),
        P(),
        P(("conf", "row"), "col"),
        P(),
        P(),
        P(),
        P(),
        P(),
    )
    out_specs = (P(("conf", "row"), "col", None), P(("conf", "row"), "col"))
    return jax.shard_map(
        functools.partial(local, mesh.shape["col"]),
        mesh=mesh,
        in_specs=in_specs,
        out_specs=out_specs,
        check_vma=False,
    )
```

```python
import functools

import jax
import jax.numpy as jnp
from jax import lax
from jax.experimental import pallas as pl
from jax.experimental.pallas import tpu as pltpu
from jax.sharding import PartitionSpec as P

EPSILON = 1e-05
LANES = 128
STORES = 4
LAG = 3
STRAIGHT = 1
BATCH = 2
MESH = pl.DeviceIdType.MESH


def project_tokens(
    depth, state_ref, index_ref, table_ref, first_weight_ref, second_weight_ref, left_ref, right_ref
):
    levels, features = table_ref.shape
    width = first_weight_ref.shape[1]
    tokens = index_ref.shape[0]
    per_tile = LANES // features
    tiles = tokens // per_tile
    packed = LANES // depth

    def iota(shape, axis):
        return lax.broadcasted_iota(jnp.int32, shape, axis)

    def indicator(inside):
        return inside.astype(jnp.float32).astype(jnp.bfloat16)

    def dot(left, right, dims):
        return lax.dot_general(left, right, (dims, ((), ())), preferred_element_type=jnp.float32)

    repeat = indicator(iota((LANES, features), 0) % features == iota((LANES, features), 1))
    wide = per_tile * levels
    repeat_levels = indicator(iota((wide, levels), 0) % levels == iota((wide, levels), 1))
    table_rows = dot(repeat_levels, table_ref[...], ((1,), (0,))).astype(jnp.bfloat16)
    table_wide = jnp.where(
        iota((wide, LANES), 0) // levels == iota((wide, LANES), 1) // features,
        dot(table_rows, repeat, ((1,), (1,))),
        0.0,
    ).astype(jnp.bfloat16)
    first_wide = dot(first_weight_ref[...], repeat, ((0,), (1,))).astype(jnp.bfloat16)
    second_wide = dot(second_weight_ref[...], repeat, ((0,), (1,))).astype(jnp.bfloat16)

    rows = width // packed * tokens
    token_of = iota((rows, LANES), 0) % tokens
    slot_of = iota((rows, LANES), 1) // features
    picks = []
    for position in range(packed):
        pick = indicator(
            iota((rows, width), 0) // tokens * packed + position == iota((rows, width), 1)
        )
        spread = dot(pick, second_wide, ((1,), (0,)))
        for tile in range(tiles):
            picks.append(
                jnp.where(token_of == tile * per_tile + slot_of, spread, 0.0).astype(jnp.bfloat16)
            )

    spread_index = indicator(
        iota((tokens, tokens * levels), 1) // levels == iota((tokens, tokens * levels), 0)
    )
    index_wide = dot(
        index_ref[...].astype(jnp.float32).astype(jnp.bfloat16), spread_index, ((0,), (0,))
    )
    level_of = (iota((depth, tokens * levels), 1) % levels).astype(jnp.float32)
    onehot = indicator(index_wide == level_of)
    lane_slot = iota((depth, LANES), 1) // features
    embedded = []
    for tile in range(tiles):
        looked = dot(onehot[:, tile * wide : (tile + 1) * wide], table_wide, ((1,), (0,)))
        state = state_ref[:, tile * LANES : (tile + 1) * LANES].astype(jnp.float32)
        value = (state + looked).astype(jnp.bfloat16).astype(jnp.float32)
        embedded.append(value.astype(jnp.bfloat16))
        stack = jnp.concatenate(
            [
                jnp.where(lane_slot == slot, value, 0.0).astype(jnp.bfloat16)
                for slot in range(per_tile)
            ],
            axis=0,
        )
        left_ref[tile] = dot(first_wide, stack, ((1,), (1,))).astype(jnp.bfloat16)

    blank = jnp.zeros((depth, LANES), jnp.bfloat16)
    parts = []
    for position in range(packed):
        for tile in range(tiles):
            parts.append(
                jnp.concatenate(
                    [embedded[tile] if place == position else blank for place in range(packed)], axis=0
                )
            )
    right = dot(
        jnp.concatenate(picks, axis=1), jnp.concatenate(parts, axis=1), ((1,), (1,))
    )
    for place in range(width // packed):
        right_ref[:, place * LANES : (place + 1) * LANES] = right[
            place * tokens : (place + 1) * tokens
        ].astype(jnp.bfloat16)


def kernel(
    ranks,
    depth,
    chunks,
    pair_hbm,
    kinds_hbm,
    first_table_hbm,
    second_table_hbm,
    state_hbm,
    index_hbm,
    align_table_hbm,
    first_weight_hbm,
    second_weight_hbm,
    outer_weight_hbm,
    outer_bias_hbm,
    mask_hbm,
    gain_hbm,
    gate_up_hbm,
    down_hbm,
    weight_hbm,
    dist_bias_hbm,
    pair_out_ref,
    dist_out_ref,
    left_ref,
    right_ref,
    left_all,
    right_all,
    outer_ref,
    outer_weight_raw,
    outer_weight_float,
    outer_weight_ref,
    pair_float,
    right_embed_ref,
    left_embed_ref,
    mirror_send,
    mirror_recv,
    own_part,
    start_ref,
    normed_ref,
    left_send_sem,
    left_recv_sem,
    right_send_sem,
    right_recv_sem,
    mirror_send_sem,
    mirror_recv_sem,
    relay_recv,
    relay_recv_sem,
    forward_send_sem,
    dist_weight_wide,
    dist_bias_wide,
    embed_all,
    pair_ref,
    kinds_ref,
    first_table_ref,
    second_table_ref,
    state_ref,
    index_ref,
    align_table_ref,
    first_weight_ref,
    second_weight_ref,
    outer_bias_ref,
    mask_ref,
    gain_ref,
    gate_up_ref,
    down_ref,
    weight_ref,
    dist_bias_ref,
    load_sem,
):
    conf = lax.axis_index("conf")
    row = lax.axis_index("row")
    col = lax.axis_index("col")
    local_groups, width, span = left_ref.shape
    local_tokens = right_ref.shape[0]
    block = pair_ref.shape[0]
    groups = left_all.shape[0]
    members = span // depth
    pairs = members * block
    hid = down_ref.shape[0]
    pitch = pair_float.shape[0] // block
    diagonal = row == col

    def load(place, source, target):
        return pltpu.make_async_copy(source, target, load_sem.at[place])

    early = [
        load(0, index_hbm, index_ref),
        load(1, state_hbm, state_ref),
        load(2, align_table_hbm, align_table_ref),
        load(3, first_weight_hbm, first_weight_ref),
        load(4, second_weight_hbm, second_weight_ref),
    ]
    later = [
        load(5, kinds_hbm, kinds_ref),
        load(6, first_table_hbm, first_table_ref),
        load(7, second_table_hbm, second_table_ref),
        load(8, weight_hbm, weight_ref),
        load(9, dist_bias_hbm, dist_bias_ref),
        load(10, outer_weight_hbm, outer_weight_raw),
    ]
    last_loads = [
        load(11, pair_hbm, pair_ref),
        load(12, outer_bias_hbm, outer_bias_ref),
        load(13, mask_hbm, mask_ref),
        load(14, gain_hbm, gain_ref),
        load(15, gate_up_hbm, gate_up_ref),
        load(16, down_hbm, down_ref),
    ]
    for copy in early:
        copy.start()

    barrier = pltpu.get_barrier_semaphore()
    for step in range(1, ranks):
        pl.semaphore_signal(
            barrier, inc=1, device_id=(conf, row, lax.rem(col + step, ranks)), device_id_type=MESH
        )
    for step in range(ranks):
        source = lax.rem(col + step, ranks)

        @pl.when(jnp.logical_or(jnp.logical_not(diagonal), source != col))
        def _():
            pl.semaphore_signal(
                barrier, inc=1, device_id=(conf, col, source), device_id_type=MESH
            )

    @pl.when(jnp.logical_not(diagonal))
    def _():
        pl.semaphore_signal(barrier, inc=1, device_id=(conf, col, row), device_id_type=MESH)

    for copy in later + last_loads:
        copy.start()
    for copy in early:
        copy.wait()
    project_tokens(
        depth, state_ref, index_ref, align_table_ref, first_weight_ref, second_weight_ref, left_ref, right_ref
    )

    @pl.when(jnp.logical_not(diagonal))
    def _():
        pl.semaphore_wait(barrier, 2 * ranks)

    @pl.when(diagonal)
    def _():
        pl.semaphore_wait(barrier, 2 * (ranks - 1))

    chips = ranks // 2
    partner = col + 1 - 2 * lax.rem(col, 2)

    def across(step):
        return lax.rem(col + 2 * step, ranks)

    def left_copy(source_ref, peer, slot, place):
        return pltpu.make_async_remote_copy(
            src_ref=source_ref,
            dst_ref=left_all.at[pl.ds(slot * local_groups, local_groups)],
            send_sem=left_send_sem.at[place],
            recv_sem=left_recv_sem.at[slot],
            device_id=(conf, row, peer),
            device_id_type=MESH,
        )

    def left_forward(step):
        slot = across(step)
        return left_copy(
            left_all.at[pl.ds(slot * local_groups, local_groups)], partner, slot, chips - 1 + step
        )

    left_sends = [left_copy(left_ref, across(step), col, step) for step in range(1, chips)]
    left_sends.append(left_copy(left_ref, partner, col, 0))
    for copy in left_sends:
        copy.start()

    def right_copy(target, slot):
        return pltpu.make_async_remote_copy(
            src_ref=right_ref,
            dst_ref=right_all.at[slot],
            send_sem=right_send_sem.at[target],
            recv_sem=right_recv_sem.at[slot],
            device_id=(conf, target, row),
            device_id_type=MESH,
        )

    for step in range(ranks):
        target = lax.rem(row + step, ranks)

        @pl.when(jnp.logical_or(jnp.logical_not(diagonal), target != row))
        def _():
            right_copy(target, col).start()

    left_all[pl.ds(col * local_groups, local_groups)] = left_ref[...]

    @pl.when(diagonal)
    def _():
        right_all[col] = right_ref[...]

    for copy in later:
        copy.wait()
    tokens = kinds_ref.shape[1]
    levels = lax.broadcasted_iota(jnp.int32, (first_table_ref.shape[0], tokens), 0)
    onehot = (levels == kinds_ref[...]).astype(jnp.float32).astype(jnp.bfloat16)
    for table_ref, embed_ref, place in (
        (first_table_ref, left_embed_ref, row),
        (second_table_ref, right_embed_ref, col),
    ):
        embed_all[...] = lax.dot_general(
            onehot, table_ref[...], (((0,), (0,)), ((), ())), preferred_element_type=jnp.float32
        )
        embed_ref[...] = embed_all[pl.ds(pl.multiple_of(place * block, block), block), :]
    bins = dist_bias_ref.shape[1]
    for place in range(2):
        dist_bias_wide[:, place * bins : (place + 1) * bins] = dist_bias_ref[...]
    dist_weight_wide[...] = jnp.zeros_like(dist_weight_wide)
    depth_of = weight_ref.shape[1]
    for place in range(2):
        dist_weight_wide[
            place * bins : (place + 1) * bins, place * depth_of : (place + 1) * depth_of
        ] = weight_ref[...]

    outer_weight_float[...] = outer_weight_raw[...].astype(jnp.float32)
    for index in range(width):
        outer_weight_ref[index * width : (index + 1) * width, :] = outer_weight_float[
            pl.ds(index, width, stride=width), :
        ].astype(jnp.bfloat16)
    for copy in last_loads:
        copy.wait()

    for step in range(1, chips):
        left_copy(left_ref, partner, across(step), 0).wait_recv()
        left_forward(step).start()
    for step in range(chips):
        left_copy(left_ref, partner, lax.rem(partner + 2 * step, ranks), 0).wait_recv()
    for step in range(ranks):
        source = lax.rem(col + step, ranks)

        @pl.when(jnp.logical_or(jnp.logical_not(diagonal), source != col))
        def _():
            right_copy(source, source).wait_recv()

    lane = lax.broadcasted_iota(jnp.int32, (width, LANES), 1)
    packed = LANES // depth
    span_tiles = span // LANES
    zero = jnp.zeros((width, LANES), jnp.bfloat16)
    spans = right_ref.shape[1] // span

    def right_rows(place):
        found = [
            right_all[source, :, place * span : (place + 1) * span] for source in range(ranks)
        ]
        if local_tokens % 16 == 0:
            return jnp.concatenate(found, axis=0)
        return jnp.concatenate([part.astype(jnp.float32) for part in found], axis=0).astype(jnp.bfloat16)

    def outer(step):
        for part in range(BATCH):
            outer_group(step * BATCH + part, part * pairs)

    def outer_group(group, offset):
        found = [
            left_all[group, :, tile * LANES : (tile + 1) * LANES].astype(jnp.float32)
            for tile in range(span_tiles)
        ]
        spread = []
        for member in range(members):
            kept = []
            for position in range(packed):
                shift = (position - member % packed) * depth % LANES
                moved = found[member // packed]
                moved = moved if shift == 0 else pltpu.roll(moved, shift, 1)
                inside = jnp.logical_and(lane >= position * depth, lane < (position + 1) * depth)
                kept.append(jnp.where(inside, moved, 0.0).astype(jnp.bfloat16))
            for place in range(members):
                spread.append(
                    jnp.concatenate(
                        [kept[place % packed] if t == place // packed else zero for t in range(span_tiles)],
                        axis=1,
                    )
                )
        rows = jnp.concatenate([right_rows(place) for place in range(spans)], axis=0)
        wide = members * width
        for first in range(0, members, 2):
            product = lax.dot_general(
                rows,
                jnp.concatenate(spread[first * members : (first + 2) * members], axis=0),
                (((1,), (1,)), ((), ())),
                preferred_element_type=jnp.float32,
            ).astype(jnp.bfloat16)
            for member in range(2):
                for place in range(spans):
                    below = offset + (first + member) * block
                    outer_ref[below : below + block, place * wide : (place + 1) * wide] = product[
                        place * block : (place + 1) * block, member * wide : (member + 1) * wide
                    ]

    far = (col // 2 == lax.rem(row // 2 + chips // 2, chips)) if chips > 1 else None
    relay = (col // 2 == row // 2) if chips > 1 else None
    relay_col = row // 2 * 2 + lax.rem(col, 2)
    served_col = lax.rem(row // 2 + chips // 2, max(chips, 1)) * 2 + lax.rem(col, 2)
    part_tiles = block // 4 // chunks

    def half_of(chunk, half):
        return pl.ds((chunk * 2 + half) * part_tiles, part_tiles)

    def mirror_copy(chunk, half):
        return pltpu.make_async_remote_copy(
            src_ref=mirror_send.at[half_of(chunk, half)],
            dst_ref=mirror_recv.at[half_of(chunk, half)],
            send_sem=mirror_send_sem.at[half, chunk],
            recv_sem=mirror_recv_sem.at[half, chunk],
            device_id=(conf, col, row),
            device_id_type=MESH,
        )

    def relay_copy(chunk, target):
        return pltpu.make_async_remote_copy(
            src_ref=mirror_send.at[half_of(chunk, 1)],
            dst_ref=relay_recv.at[chunk],
            send_sem=mirror_send_sem.at[1, chunk],
            recv_sem=relay_recv_sem.at[chunk],
            device_id=(conf, row, target),
            device_id_type=MESH,
        )

    def forward_copy(chunk):
        return pltpu.make_async_remote_copy(
            src_ref=relay_recv.at[chunk],
            dst_ref=mirror_recv.at[half_of(chunk, 1)],
            send_sem=forward_send_sem.at[chunk],
            recv_sem=mirror_recv_sem.at[1, chunk],
            device_id=(conf, served_col, row),
            device_id_type=MESH,
        )

    def send_chunk(chunk):
        @pl.when(jnp.logical_not(diagonal))
        def _():
            mirror_copy(chunk, 0).start()

        if chips > 1:
            routed = jnp.logical_and(far, chunk < chunks - STRAIGHT)

            @pl.when(routed)
            def _():
                relay_copy(chunk, relay_col).start()

            @pl.when(jnp.logical_not(jnp.logical_or(diagonal, routed)))
            def _():
                mirror_copy(chunk, 1).start()
        else:

            @pl.when(jnp.logical_not(diagonal))
            def _():
                mirror_copy(chunk, 1).start()

    def pass_on(chunk):
        relay_copy(chunk, served_col).wait_recv()
        forward_copy(chunk).start()

    mask_rows, mask_cols = mask_ref.shape
    batch_members = BATCH * members
    steps = groups // BATCH
    steps_per_mask = steps // mask_rows
    mask_side = block // mask_cols
    tiles = block // 2 // chunks
    channels = pair_ref.shape[2]

    def project():
        return jnp.dot(outer_ref[...], outer_weight_ref[...], preferred_element_type=jnp.float32)

    def normalise(step, summed):
        update = summed * (1.0 / depth) + outer_bias_ref[...].astype(jnp.float32)
        mask_col = jnp.concatenate(
            [
                jnp.full(
                    (mask_side, channels),
                    mask_ref[step // steps_per_mask, place].astype(jnp.float32),
                    jnp.float32,
                )
                for place in range(mask_cols)
            ],
            axis=0,
        )
        first = pl.multiple_of(step * batch_members, batch_members)
        state = pair_ref[pl.ds(first, batch_members)].astype(jnp.float32)
        left_embed = left_embed_ref[pl.ds(first, batch_members), :]
        start = (
            state
            + left_embed[:, None, :]
            + right_embed_ref[...][None]
            + mask_col[None] * update.reshape(batch_members, block, channels)
        ).reshape(BATCH * pairs, channels)
        mean = jnp.mean(start, axis=-1, keepdims=True)
        centered = start - mean
        variance = jnp.mean(centered * centered, axis=-1, keepdims=True)
        normed = (centered * lax.rsqrt(variance + EPSILON) * gain_ref[...]).astype(jnp.bfloat16)
        return start, normed

    def expand(normed):
        hidden = []
        for place in range(0, hid, LANES):
            weight = jnp.concatenate(
                [
                    gate_up_ref[:, place : place + LANES],
                    gate_up_ref[:, hid + place : hid + place + LANES],
                ],
                axis=1,
            )
            gate_up = jnp.dot(normed, weight, preferred_element_type=jnp.float32)
            half = 0.5 * gate_up[:, :LANES]
            hidden.append(((half + half * jnp.tanh(half)) * gate_up[:, LANES:]).astype(jnp.bfloat16))
        return jnp.concatenate(hidden, axis=1)

    def contract(start, hidden):
        branch = jnp.dot(hidden, down_ref[...], preferred_element_type=jnp.float32)
        result = (start + branch).astype(jnp.bfloat16)
        shaped = result.reshape(batch_members // 2, 2, block, channels)
        joined = jnp.concatenate([shaped[:, 0], shaped[:, 1]], axis=-1).reshape(
            batch_members // 2 * block, 2 * channels
        )
        part = lax.dot_general(
            joined, dist_weight_wide[...], (((1,), (1,)), ((), ())),
            preferred_element_type=jnp.float32,
        )
        return result, part.astype(jnp.bfloat16).reshape(batch_members // 2, block, LANES)

    last = steps - 1
    outer(0)
    start_ref[...], normed_ref[...] = normalise(0, project())
    outer(1)

    def group_step(step, carry):
        start = start_ref[...]
        hidden = expand(normed_ref[...])
        summed = project()
        result, part = contract(start, hidden)
        next_start, next_normed = normalise(jnp.minimum(step + 1, last), summed)
        outer(jnp.minimum(step + 2, last))
        first = pl.multiple_of(step * batch_members, batch_members)
        pair_out_ref[pl.ds(first, batch_members)] = result.reshape(batch_members, block, channels)
        wide = result.astype(jnp.float32)
        for member in range(batch_members):
            pair_float[pl.ds((first + member) * pitch, block), :] = wide[
                member * block : (member + 1) * block
            ]
        mirror_send[pl.ds(step * (batch_members // 2), batch_members // 2)] = part
        start_ref[...] = next_start
        normed_ref[...] = next_normed
        return carry

    steps_per_chunk = steps // chunks

    def chunk_step(chunk, carry):
        lax.fori_loop(chunk * steps_per_chunk, (chunk + 1) * steps_per_chunk, group_step, 0)

        send_chunk(chunk)
        if chips > 1:

            @pl.when(jnp.logical_and(relay, chunk >= LAG))
            def _():
                pass_on(chunk - LAG)

        return carry

    lax.fori_loop(0, chunks, chunk_step, 0)

    if chips > 1:

        @pl.when(relay)
        def _():
            for chunk in range(chunks - LAG, chunks - STRAIGHT):
                pass_on(chunk)

    def own_step(tile, carry):
        even = pair_float[pl.ds(2 * tile, block, stride=pitch), :]
        odd = pair_float[pl.ds(2 * tile + 1, block, stride=pitch), :]
        joined = jnp.concatenate([even, odd], axis=1).astype(jnp.bfloat16)
        part = lax.dot_general(
            joined, dist_weight_wide[...], (((1,), (1,)), ((), ())),
            preferred_element_type=jnp.float32,
        )
        own_part[tile] = part.astype(jnp.bfloat16).astype(jnp.float32) + dist_bias_wide[...]
        return carry

    lax.fori_loop(0, block // 2, own_step, 0, unroll=4)

    def finish(tiles_from):
        def step(chunk, carry):
            @pl.when(jnp.logical_not(diagonal))
            def _():
                mirror_copy(chunk, 0).wait_recv()
                mirror_copy(chunk, 1).wait_recv()

            for tile in range(tiles):
                index = chunk * tiles + tile
                total = own_part[index] + tiles_from[index].astype(jnp.float32)
                dist_out_ref[:, pl.ds(pl.multiple_of(index * LANES, LANES), LANES)] = total.astype(
                    jnp.bfloat16
                )
            return carry

        lax.fori_loop(0, chunks, step, 0)

    @pl.when(diagonal)
    def _():
        finish(mirror_send)

    @pl.when(jnp.logical_not(diagonal))
    def _():
        finish(mirror_recv)
        for chunk in range(chunks):
            mirror_copy(chunk, 0).wait_send()
            mirror_copy(chunk, 1).wait_send()

    if chips > 1:

        @pl.when(relay)
        def _():
            for chunk in range(chunks - STRAIGHT):
                forward_copy(chunk).wait_send()

    for step in range(ranks):
        target = lax.rem(row + step, ranks)

        @pl.when(jnp.logical_or(jnp.logical_not(diagonal), target != row))
        def _():
            right_copy(target, col).wait_send()

    for copy in left_sends:
        copy.wait_send()
    for step in range(1, chips):
        left_forward(step).wait_send()


def store(pair_ref, dist_ref, pair_hbm, dist_hbm, store_sem):
    copies = []
    for place, (source, target) in enumerate(((pair_ref, pair_hbm), (dist_ref, dist_hbm))):
        rows = source.shape[0] // STORES
        for part in range(STORES):
            span = pl.ds(part * rows, rows)
            copies.append(
                pltpu.make_async_copy(source.at[span], target.at[span], store_sem.at[place, part])
            )
    for copy in copies:
        copy.start()
    for copy in copies:
        copy.wait()


def local(
    ranks,
    pair_state,
    token_kinds,
    first_type_table,
    second_type_table,
    alignment_state,
    alignment_index,
    alignment_table,
    first_weight,
    second_weight,
    outer_product_weight,
    outer_product_bias,
    pair_block_mask,
    transition_gain,
    transition_gate_up,
    transition_down,
    distance_weight,
    distance_bias,
):
    block = pair_state.shape[0]
    channels = pair_state.shape[2]
    depth, local_tokens = alignment_index.shape
    features = alignment_state.shape[1] // local_tokens
    width = first_weight.shape[1]
    bins = distance_weight.shape[1]
    members = 2 * LANES // depth
    groups = block // members
    local_groups = local_tokens // members
    chunks = block // (BATCH * members)

    vmem = pl.BlockSpec(memory_space=pltpu.VMEM)
    hbm = pl.BlockSpec(memory_space=pltpu.HBM)
    pair_out, distogram = pl.pallas_call(
        functools.partial(kernel, ranks, depth, chunks),
        out_shape=(
            pltpu.VMEM(pair_state.shape, jnp.bfloat16),
            pltpu.VMEM((block, block * bins), jnp.bfloat16),
        ),
        in_specs=[hbm] * 17,
        out_specs=(vmem, vmem),
        scratch_shapes=[
            pltpu.VMEM((local_groups, width, members * depth), jnp.bfloat16),
            pltpu.VMEM((local_tokens, width * depth), jnp.bfloat16),
            pltpu.VMEM((groups, width, members * depth), jnp.bfloat16),
            pltpu.VMEM((ranks, local_tokens, width * depth), jnp.bfloat16),
            pltpu.VMEM((BATCH * members * block, width * width), jnp.bfloat16),
            pltpu.VMEM(outer_product_weight.shape, jnp.bfloat16),
            pltpu.VMEM(outer_product_weight.shape, jnp.float32),
            pltpu.VMEM(outer_product_weight.shape, jnp.bfloat16),
            pltpu.VMEM((block * (block + 1), channels), jnp.float32),
            pltpu.VMEM((block, channels), jnp.float32),
            pltpu.VMEM((block, channels), jnp.float32),
            pltpu.VMEM((block // 2, block, 2 * bins), jnp.bfloat16),
            pltpu.VMEM((block // 2, block, 2 * bins), jnp.bfloat16),
            pltpu.VMEM((block // 2, block, 2 * bins), jnp.float32),
            pltpu.VMEM((BATCH * members * block, channels), jnp.float32),
            pltpu.VMEM((BATCH * members * block, channels), jnp.bfloat16),
            pltpu.SemaphoreType.DMA((ranks,)),
            pltpu.SemaphoreType.DMA((ranks,)),
            pltpu.SemaphoreType.DMA((ranks,)),
            pltpu.SemaphoreType.DMA((ranks,)),
            pltpu.SemaphoreType.DMA((2, chunks)),
            pltpu.SemaphoreType.DMA((2, chunks)),
            pltpu.VMEM((chunks, block // 4 // chunks, block, 2 * bins), jnp.bfloat16),
            pltpu.SemaphoreType.DMA((chunks,)),
            pltpu.SemaphoreType.DMA((chunks,)),
            pltpu.VMEM((2 * bins, 2 * channels), jnp.bfloat16),
            pltpu.VMEM((1, 2 * bins), jnp.float32),
            pltpu.VMEM((token_kinds.shape[0], channels), jnp.float32),
            pltpu.VMEM(pair_state.shape, pair_state.dtype),
            pltpu.VMEM((1, token_kinds.shape[0]), jnp.int32),
            pltpu.VMEM(first_type_table.shape, jnp.bfloat16),
            pltpu.VMEM(second_type_table.shape, jnp.bfloat16),
            pltpu.VMEM(alignment_state.shape, jnp.bfloat16),
            pltpu.VMEM((local_tokens, depth), jnp.int32),
            pltpu.VMEM(alignment_table.shape, jnp.bfloat16),
            pltpu.VMEM(first_weight.shape, jnp.bfloat16),
            pltpu.VMEM(second_weight.shape, jnp.bfloat16),
            pltpu.VMEM((1, channels), jnp.bfloat16),
            pltpu.SMEM(pair_block_mask.shape, jnp.int32),
            pltpu.VMEM((1, channels), jnp.float32),
            pltpu.VMEM(transition_gate_up.shape, transition_gate_up.dtype),
            pltpu.VMEM(transition_down.shape, transition_down.dtype),
            pltpu.VMEM((bins, channels), jnp.bfloat16),
            pltpu.VMEM((1, bins), jnp.float32),
            pltpu.SemaphoreType.DMA((17,)),
        ],
        compiler_params=pltpu.CompilerParams(
            collective_id=0,
            has_side_effects=True,
            vmem_limit_bytes=56 * 1024 * 1024,
        ),
    )(
        pair_state,
        token_kinds[None],
        first_type_table,
        second_type_table,
        alignment_state,
        alignment_index.T,
        alignment_table,
        first_weight,
        second_weight,
        outer_product_weight,
        outer_product_bias[None],
        pair_block_mask,
        transition_gain[None],
        transition_gate_up,
        transition_down,
        distance_weight.T,
        distance_bias[None],
    )
    return pl.pallas_call(
        store,
        out_shape=(
            jax.ShapeDtypeStruct(pair_state.shape, jnp.bfloat16),
            jax.ShapeDtypeStruct((block, block * bins), jnp.bfloat16),
        ),
        in_specs=[vmem, vmem],
        out_specs=(hbm, hbm),
        scratch_shapes=[pltpu.SemaphoreType.DMA((2, STORES))],
    )(
        pltpu.with_memory_space_constraint(pair_out, pltpu.VMEM),
        pltpu.with_memory_space_constraint(distogram, pltpu.VMEM),
    )


def solution(mesh):
    in_specs = (
        P(("conf", "row"), "col", None),
        P("conf"),
        P(),
        P(),
        P(None, ("conf", "row", "col")),
        P(None, ("conf", "row", "col")),
        P(),
        P(),
        P(),
        P(),
        P(),
        P(("conf", "row"), "col"),
        P(),
        P(),
        P(),
        P(),
        P(),
    )
    out_specs = (P(("conf", "row"), "col", None), P(("conf", "row"), "col"))
    return jax.shard_map(
        functools.partial(local, mesh.shape["col"]),
        mesh=mesh,
        in_specs=in_specs,
        out_specs=out_specs,
        check_vma=False,
    )
```

```python
import functools

import jax
import jax.numpy as jnp
from jax import lax
from jax.experimental import pallas as pl
from jax.experimental.pallas import tpu as pltpu
from jax.sharding import PartitionSpec as P

EPSILON = 1e-05
LANES = 128
STORES = 4
LAG = 3
STRAIGHT = 1
BATCH = 2
MESH = pl.DeviceIdType.MESH


def project_tokens(
    depth, state_ref, index_ref, table_ref, first_weight_ref, second_weight_ref, left_ref, right_ref
):
    levels, features = table_ref.shape
    width = first_weight_ref.shape[1]
    tokens = index_ref.shape[0]
    per_tile = LANES // features
    tiles = tokens // per_tile
    packed = LANES // depth

    def iota(shape, axis):
        return lax.broadcasted_iota(jnp.int32, shape, axis)

    def indicator(inside):
        return inside.astype(jnp.float32).astype(jnp.bfloat16)

    def dot(left, right, dims):
        return lax.dot_general(left, right, (dims, ((), ())), preferred_element_type=jnp.float32)

    repeat = indicator(iota((LANES, features), 0) % features == iota((LANES, features), 1))
    wide = per_tile * levels
    repeat_levels = indicator(iota((wide, levels), 0) % levels == iota((wide, levels), 1))
    table_rows = dot(repeat_levels, table_ref[...], ((1,), (0,))).astype(jnp.bfloat16)
    table_wide = jnp.where(
        iota((wide, LANES), 0) // levels == iota((wide, LANES), 1) // features,
        dot(table_rows, repeat, ((1,), (1,))),
        0.0,
    ).astype(jnp.bfloat16)
    first_wide = dot(first_weight_ref[...], repeat, ((0,), (1,))).astype(jnp.bfloat16)
    second_wide = dot(second_weight_ref[...], repeat, ((0,), (1,))).astype(jnp.bfloat16)

    rows = width // packed * tokens
    token_of = iota((rows, LANES), 0) % tokens
    slot_of = iota((rows, LANES), 1) // features
    picks = []
    for position in range(packed):
        pick = indicator(
            iota((rows, width), 0) // tokens * packed + position == iota((rows, width), 1)
        )
        spread = dot(pick, second_wide, ((1,), (0,)))
        for tile in range(tiles):
            picks.append(
                jnp.where(token_of == tile * per_tile + slot_of, spread, 0.0).astype(jnp.bfloat16)
            )

    spread_index = indicator(
        iota((tokens, tokens * levels), 1) // levels == iota((tokens, tokens * levels), 0)
    )
    index_wide = dot(
        index_ref[...].astype(jnp.float32).astype(jnp.bfloat16), spread_index, ((0,), (0,))
    )
    level_of = (iota((depth, tokens * levels), 1) % levels).astype(jnp.float32)
    onehot = indicator(index_wide == level_of)
    lane_slot = iota((depth, LANES), 1) // features
    embedded = []
    for tile in range(tiles):
        looked = dot(onehot[:, tile * wide : (tile + 1) * wide], table_wide, ((1,), (0,)))
        state = state_ref[:, tile * LANES : (tile + 1) * LANES].astype(jnp.float32)
        value = (state + looked).astype(jnp.bfloat16).astype(jnp.float32)
        embedded.append(value.astype(jnp.bfloat16))
        stack = jnp.concatenate(
            [
                jnp.where(lane_slot == slot, value, 0.0).astype(jnp.bfloat16)
                for slot in range(per_tile)
            ],
            axis=0,
        )
        left_ref[tile] = dot(first_wide, stack, ((1,), (1,))).astype(jnp.bfloat16)

    blank = jnp.zeros((depth, LANES), jnp.bfloat16)
    parts = []
    for position in range(packed):
        for tile in range(tiles):
            parts.append(
                jnp.concatenate(
                    [embedded[tile] if place == position else blank for place in range(packed)], axis=0
                )
            )
    right = dot(
        jnp.concatenate(picks, axis=1), jnp.concatenate(parts, axis=1), ((1,), (1,))
    )
    for place in range(width // packed):
        right_ref[:, place * LANES : (place + 1) * LANES] = right[
            place * tokens : (place + 1) * tokens
        ].astype(jnp.bfloat16)


def kernel(
    ranks,
    depth,
    chunks,
    pair_hbm,
    kinds_hbm,
    first_table_hbm,
    second_table_hbm,
    state_hbm,
    index_hbm,
    align_table_hbm,
    first_weight_hbm,
    second_weight_hbm,
    outer_weight_hbm,
    outer_bias_hbm,
    mask_hbm,
    gain_hbm,
    gate_up_hbm,
    down_hbm,
    weight_hbm,
    dist_bias_hbm,
    pair_out_ref,
    dist_out_ref,
    left_ref,
    right_ref,
    left_all,
    right_all,
    outer_ref,
    outer_weight_raw,
    outer_weight_float,
    outer_weight_ref,
    pair_float,
    right_embed_ref,
    left_embed_ref,
    mirror_send,
    mirror_recv,
    own_part,
    start_ref,
    normed_ref,
    left_send_sem,
    left_recv_sem,
    right_send_sem,
    right_recv_sem,
    mirror_send_sem,
    mirror_recv_sem,
    relay_recv,
    relay_recv_sem,
    forward_send_sem,
    dist_weight_wide,
    dist_bias_wide,
    embed_all,
    pair_ref,
    kinds_ref,
    first_table_ref,
    second_table_ref,
    state_ref,
    index_ref,
    align_table_ref,
    first_weight_ref,
    second_weight_ref,
    outer_bias_ref,
    mask_ref,
    gain_ref,
    gate_up_ref,
    down_ref,
    weight_ref,
    dist_bias_ref,
    load_sem,
):
    conf = lax.axis_index("conf")
    row = lax.axis_index("row")
    col = lax.axis_index("col")
    local_groups, width, span = left_ref.shape
    local_tokens = right_ref.shape[0]
    block = pair_ref.shape[0]
    groups = left_all.shape[0]
    members = span // depth
    pairs = members * block
    hid = down_ref.shape[0]
    pitch = pair_float.shape[0] // block
    diagonal = row == col

    def load(place, source, target):
        return pltpu.make_async_copy(source, target, load_sem.at[place])

    early = [
        load(0, index_hbm, index_ref),
        load(1, state_hbm, state_ref),
        load(2, align_table_hbm, align_table_ref),
        load(3, first_weight_hbm, first_weight_ref),
        load(4, second_weight_hbm, second_weight_ref),
    ]
    later = [
        load(5, kinds_hbm, kinds_ref),
        load(6, first_table_hbm, first_table_ref),
        load(7, second_table_hbm, second_table_ref),
        load(8, weight_hbm, weight_ref),
        load(9, dist_bias_hbm, dist_bias_ref),
        load(10, outer_weight_hbm, outer_weight_raw),
    ]
    last_loads = [
        load(11, pair_hbm, pair_ref),
        load(12, outer_bias_hbm, outer_bias_ref),
        load(13, mask_hbm, mask_ref),
        load(14, gain_hbm, gain_ref),
        load(15, gate_up_hbm, gate_up_ref),
        load(16, down_hbm, down_ref),
    ]
    for copy in early:
        copy.start()

    barrier = pltpu.get_barrier_semaphore()
    for step in range(1, ranks):
        pl.semaphore_signal(
            barrier, inc=1, device_id=(conf, row, lax.rem(col + step, ranks)), device_id_type=MESH
        )
    for step in range(ranks):
        source = lax.rem(col + step, ranks)

        @pl.when(jnp.logical_or(jnp.logical_not(diagonal), source != col))
        def _():
            pl.semaphore_signal(
                barrier, inc=1, device_id=(conf, col, source), device_id_type=MESH
            )

    @pl.when(jnp.logical_not(diagonal))
    def _():
        pl.semaphore_signal(barrier, inc=1, device_id=(conf, col, row), device_id_type=MESH)

    for copy in later + last_loads:
        copy.start()
    for copy in early:
        copy.wait()
    project_tokens(
        depth, state_ref, index_ref, align_table_ref, first_weight_ref, second_weight_ref, left_ref, right_ref
    )

    @pl.when(jnp.logical_not(diagonal))
    def _():
        pl.semaphore_wait(barrier, 2 * ranks)

    @pl.when(diagonal)
    def _():
        pl.semaphore_wait(barrier, 2 * (ranks - 1))

    chips = ranks // 2
    partner = col + 1 - 2 * lax.rem(col, 2)

    def across(step):
        return lax.rem(col + 2 * step, ranks)

    def left_copy(source_ref, peer, slot, place):
        return pltpu.make_async_remote_copy(
            src_ref=source_ref,
            dst_ref=left_all.at[pl.ds(slot * local_groups, local_groups)],
            send_sem=left_send_sem.at[place],
            recv_sem=left_recv_sem.at[slot],
            device_id=(conf, row, peer),
            device_id_type=MESH,
        )

    def left_forward(step):
        slot = across(step)
        return left_copy(
            left_all.at[pl.ds(slot * local_groups, local_groups)], partner, slot, chips - 1 + step
        )

    left_sends = [left_copy(left_ref, across(step), col, step) for step in range(1, chips)]
    left_sends.append(left_copy(left_ref, partner, col, 0))
    for copy in left_sends:
        copy.start()

    def right_copy(target, slot):
        return pltpu.make_async_remote_copy(
            src_ref=right_ref,
            dst_ref=right_all.at[slot],
            send_sem=right_send_sem.at[target],
            recv_sem=right_recv_sem.at[slot],
            device_id=(conf, target, row),
            device_id_type=MESH,
        )

    for step in range(ranks):
        target = jnp.where(row < ranks // 2, ranks - 1 - step, step)

        @pl.when(jnp.logical_or(jnp.logical_not(diagonal), target != row))
        def _():
            right_copy(target, col).start()

    left_all[pl.ds(col * local_groups, local_groups)] = left_ref[...]

    @pl.when(diagonal)
    def _():
        right_all[col] = right_ref[...]

    for copy in later:
        copy.wait()
    tokens = kinds_ref.shape[1]
    levels = lax.broadcasted_iota(jnp.int32, (first_table_ref.shape[0], tokens), 0)
    onehot = (levels == kinds_ref[...]).astype(jnp.float32).astype(jnp.bfloat16)
    for table_ref, embed_ref, place in (
        (first_table_ref, left_embed_ref, row),
        (second_table_ref, right_embed_ref, col),
    ):
        embed_all[...] = lax.dot_general(
            onehot, table_ref[...], (((0,), (0,)), ((), ())), preferred_element_type=jnp.float32
        )
        embed_ref[...] = embed_all[pl.ds(pl.multiple_of(place * block, block), block), :]
    bins = dist_bias_ref.shape[1]
    for place in range(2):
        dist_bias_wide[:, place * bins : (place + 1) * bins] = dist_bias_ref[...]
    dist_weight_wide[...] = jnp.zeros_like(dist_weight_wide)
    depth_of = weight_ref.shape[1]
    for place in range(2):
        dist_weight_wide[
            place * bins : (place + 1) * bins, place * depth_of : (place + 1) * depth_of
        ] = weight_ref[...]

    outer_weight_float[...] = outer_weight_raw[...].astype(jnp.float32)
    for index in range(width):
        outer_weight_ref[index * width : (index + 1) * width, :] = outer_weight_float[
            pl.ds(index, width, stride=width), :
        ].astype(jnp.bfloat16)
    for copy in last_loads:
        copy.wait()

    for step in range(1, chips):
        left_copy(left_ref, partner, across(step), 0).wait_recv()
        left_forward(step).start()
    for step in range(chips):
        left_copy(left_ref, partner, lax.rem(partner + 2 * step, ranks), 0).wait_recv()
    for step in range(ranks):
        source = lax.rem(col + step, ranks)

        @pl.when(jnp.logical_or(jnp.logical_not(diagonal), source != col))
        def _():
            right_copy(source, source).wait_recv()

    lane = lax.broadcasted_iota(jnp.int32, (width, LANES), 1)
    packed = LANES // depth
    span_tiles = span // LANES
    zero = jnp.zeros((width, LANES), jnp.bfloat16)
    spans = right_ref.shape[1] // span

    def right_rows(place):
        found = [
            right_all[source, :, place * span : (place + 1) * span] for source in range(ranks)
        ]
        if local_tokens % 16 == 0:
            return jnp.concatenate(found, axis=0)
        return jnp.concatenate([part.astype(jnp.float32) for part in found], axis=0).astype(jnp.bfloat16)

    def outer(step):
        for part in range(BATCH):
            outer_group(step * BATCH + part, part * pairs)

    def outer_group(group, offset):
        found = [
            left_all[group, :, tile * LANES : (tile + 1) * LANES].astype(jnp.float32)
            for tile in range(span_tiles)
        ]
        spread = []
        for member in range(members):
            kept = []
            for position in range(packed):
                shift = (position - member % packed) * depth % LANES
                moved = found[member // packed]
                moved = moved if shift == 0 else pltpu.roll(moved, shift, 1)
                inside = jnp.logical_and(lane >= position * depth, lane < (position + 1) * depth)
                kept.append(jnp.where(inside, moved, 0.0).astype(jnp.bfloat16))
            for place in range(members):
                spread.append(
                    jnp.concatenate(
                        [kept[place % packed] if t == place // packed else zero for t in range(span_tiles)],
                        axis=1,
                    )
                )
        rows = jnp.concatenate([right_rows(place) for place in range(spans)], axis=0)
        wide = members * width
        for first in range(0, members, 2):
            product = lax.dot_general(
                rows,
                jnp.concatenate(spread[first * members : (first + 2) * members], axis=0),
                (((1,), (1,)), ((), ())),
                preferred_element_type=jnp.float32,
            ).astype(jnp.bfloat16)
            for member in range(2):
                for place in range(spans):
                    below = offset + (first + member) * block
                    outer_ref[below : below + block, place * wide : (place + 1) * wide] = product[
                        place * block : (place + 1) * block, member * wide : (member + 1) * wide
                    ]

    far = (col // 2 == lax.rem(row // 2 + chips // 2, chips)) if chips > 1 else None
    relay = (col // 2 == row // 2) if chips > 1 else None
    relay_col = row // 2 * 2 + lax.rem(col, 2)
    served_col = lax.rem(row // 2 + chips // 2, max(chips, 1)) * 2 + lax.rem(col, 2)
    part_tiles = block // 4 // chunks

    def half_of(chunk, half):
        return pl.ds((chunk * 2 + half) * part_tiles, part_tiles)

    def mirror_copy(chunk, half):
        return pltpu.make_async_remote_copy(
            src_ref=mirror_send.at[half_of(chunk, half)],
            dst_ref=mirror_recv.at[half_of(chunk, half)],
            send_sem=mirror_send_sem.at[half, chunk],
            recv_sem=mirror_recv_sem.at[half, chunk],
            device_id=(conf, col, row),
            device_id_type=MESH,
        )

    def relay_copy(chunk, target):
        return pltpu.make_async_remote_copy(
            src_ref=mirror_send.at[half_of(chunk, 1)],
            dst_ref=relay_recv.at[chunk],
            send_sem=mirror_send_sem.at[1, chunk],
            recv_sem=relay_recv_sem.at[chunk],
            device_id=(conf, row, target),
            device_id_type=MESH,
        )

    def forward_copy(chunk):
        return pltpu.make_async_remote_copy(
            src_ref=relay_recv.at[chunk],
            dst_ref=mirror_recv.at[half_of(chunk, 1)],
            send_sem=forward_send_sem.at[chunk],
            recv_sem=mirror_recv_sem.at[1, chunk],
            device_id=(conf, served_col, row),
            device_id_type=MESH,
        )

    def send_chunk(chunk):
        @pl.when(jnp.logical_not(diagonal))
        def _():
            mirror_copy(chunk, 0).start()

        if chips > 1:
            routed = jnp.logical_and(far, chunk < chunks - STRAIGHT)

            @pl.when(routed)
            def _():
                relay_copy(chunk, relay_col).start()

            @pl.when(jnp.logical_not(jnp.logical_or(diagonal, routed)))
            def _():
                mirror_copy(chunk, 1).start()
        else:

            @pl.when(jnp.logical_not(diagonal))
            def _():
                mirror_copy(chunk, 1).start()

    def pass_on(chunk):
        relay_copy(chunk, served_col).wait_recv()
        forward_copy(chunk).start()

    mask_rows, mask_cols = mask_ref.shape
    batch_members = BATCH * members
    steps = groups // BATCH
    steps_per_mask = steps // mask_rows
    mask_side = block // mask_cols
    tiles = block // 2 // chunks
    channels = pair_ref.shape[2]

    def project():
        return jnp.dot(outer_ref[...], outer_weight_ref[...], preferred_element_type=jnp.float32)

    def normalise(step, summed):
        update = summed * (1.0 / depth) + outer_bias_ref[...].astype(jnp.float32)
        mask_col = jnp.concatenate(
            [
                jnp.full(
                    (mask_side, channels),
                    mask_ref[step // steps_per_mask, place].astype(jnp.float32),
                    jnp.float32,
                )
                for place in range(mask_cols)
            ],
            axis=0,
        )
        first = pl.multiple_of(step * batch_members, batch_members)
        state = pair_ref[pl.ds(first, batch_members)].astype(jnp.float32)
        left_embed = left_embed_ref[pl.ds(first, batch_members), :]
        start = (
            state
            + left_embed[:, None, :]
            + right_embed_ref[...][None]
            + mask_col[None] * update.reshape(batch_members, block, channels)
        ).reshape(BATCH * pairs, channels)
        mean = jnp.mean(start, axis=-1, keepdims=True)
        centered = start - mean
        variance = jnp.mean(centered * centered, axis=-1, keepdims=True)
        normed = (centered * lax.rsqrt(variance + EPSILON) * gain_ref[...]).astype(jnp.bfloat16)
        return start, normed

    def expand(normed):
        hidden = []
        for place in range(0, hid, LANES):
            weight = jnp.concatenate(
                [
                    gate_up_ref[:, place : place + LANES],
                    gate_up_ref[:, hid + place : hid + place + LANES],
                ],
                axis=1,
            )
            gate_up = jnp.dot(normed, weight, preferred_element_type=jnp.float32)
            half = 0.5 * gate_up[:, :LANES]
            hidden.append(((half + half * jnp.tanh(half)) * gate_up[:, LANES:]).astype(jnp.bfloat16))
        return jnp.concatenate(hidden, axis=1)

    def contract(start, hidden):
        branch = jnp.dot(hidden, down_ref[...], preferred_element_type=jnp.float32)
        result = (start + branch).astype(jnp.bfloat16)
        shaped = result.reshape(batch_members // 2, 2, block, channels)
        joined = jnp.concatenate([shaped[:, 0], shaped[:, 1]], axis=-1).reshape(
            batch_members // 2 * block, 2 * channels
        )
        part = lax.dot_general(
            joined, dist_weight_wide[...], (((1,), (1,)), ((), ())),
            preferred_element_type=jnp.float32,
        )
        return result, part.astype(jnp.bfloat16).reshape(batch_members // 2, block, LANES)

    last = steps - 1
    outer(0)
    start_ref[...], normed_ref[...] = normalise(0, project())
    outer(1)

    def group_step(step, carry):
        start = start_ref[...]
        hidden = expand(normed_ref[...])
        summed = project()
        result, part = contract(start, hidden)
        next_start, next_normed = normalise(jnp.minimum(step + 1, last), summed)
        outer(jnp.minimum(step + 2, last))
        first = pl.multiple_of(step * batch_members, batch_members)
        pair_out_ref[pl.ds(first, batch_members)] = result.reshape(batch_members, block, channels)
        wide = result.astype(jnp.float32)
        for member in range(batch_members):
            pair_float[pl.ds((first + member) * pitch, block), :] = wide[
                member * block : (member + 1) * block
            ]
        mirror_send[pl.ds(step * (batch_members // 2), batch_members // 2)] = part
        start_ref[...] = next_start
        normed_ref[...] = next_normed
        return carry

    steps_per_chunk = steps // chunks

    def chunk_step(chunk, carry):
        lax.fori_loop(chunk * steps_per_chunk, (chunk + 1) * steps_per_chunk, group_step, 0)

        send_chunk(chunk)
        if chips > 1:

            @pl.when(jnp.logical_and(relay, chunk >= LAG))
            def _():
                pass_on(chunk - LAG)

        return carry

    lax.fori_loop(0, chunks, chunk_step, 0)

    if chips > 1:

        @pl.when(relay)
        def _():
            for chunk in range(chunks - LAG, chunks - STRAIGHT):
                pass_on(chunk)

    def own_step(tile, carry):
        even = pair_float[pl.ds(2 * tile, block, stride=pitch), :]
        odd = pair_float[pl.ds(2 * tile + 1, block, stride=pitch), :]
        joined = jnp.concatenate([even, odd], axis=1).astype(jnp.bfloat16)
        part = lax.dot_general(
            joined, dist_weight_wide[...], (((1,), (1,)), ((), ())),
            preferred_element_type=jnp.float32,
        )
        own_part[tile] = part.astype(jnp.bfloat16).astype(jnp.float32) + dist_bias_wide[...]
        return carry

    lax.fori_loop(0, block // 2, own_step, 0, unroll=4)

    def finish(tiles_from):
        def step(chunk, carry):
            @pl.when(jnp.logical_not(diagonal))
            def _():
                mirror_copy(chunk, 0).wait_recv()
                mirror_copy(chunk, 1).wait_recv()

            for tile in range(tiles):
                index = chunk * tiles + tile
                total = own_part[index] + tiles_from[index].astype(jnp.float32)
                dist_out_ref[:, pl.ds(pl.multiple_of(index * LANES, LANES), LANES)] = total.astype(
                    jnp.bfloat16
                )
            return carry

        lax.fori_loop(0, chunks, step, 0)

    @pl.when(diagonal)
    def _():
        finish(mirror_send)

    @pl.when(jnp.logical_not(diagonal))
    def _():
        finish(mirror_recv)
        for chunk in range(chunks):
            mirror_copy(chunk, 0).wait_send()
            mirror_copy(chunk, 1).wait_send()

    if chips > 1:

        @pl.when(relay)
        def _():
            for chunk in range(chunks - STRAIGHT):
                forward_copy(chunk).wait_send()

    for step in range(ranks):
        target = lax.rem(row + step, ranks)

        @pl.when(jnp.logical_or(jnp.logical_not(diagonal), target != row))
        def _():
            right_copy(target, col).wait_send()

    for copy in left_sends:
        copy.wait_send()
    for step in range(1, chips):
        left_forward(step).wait_send()


def store(pair_ref, dist_ref, pair_hbm, dist_hbm, store_sem):
    copies = []
    for place, (source, target) in enumerate(((pair_ref, pair_hbm), (dist_ref, dist_hbm))):
        rows = source.shape[0] // STORES
        for part in range(STORES):
            span = pl.ds(part * rows, rows)
            copies.append(
                pltpu.make_async_copy(source.at[span], target.at[span], store_sem.at[place, part])
            )
    for copy in copies:
        copy.start()
    for copy in copies:
        copy.wait()


def local(
    ranks,
    pair_state,
    token_kinds,
    first_type_table,
    second_type_table,
    alignment_state,
    alignment_index,
    alignment_table,
    first_weight,
    second_weight,
    outer_product_weight,
    outer_product_bias,
    pair_block_mask,
    transition_gain,
    transition_gate_up,
    transition_down,
    distance_weight,
    distance_bias,
):
    block = pair_state.shape[0]
    channels = pair_state.shape[2]
    depth, local_tokens = alignment_index.shape
    features = alignment_state.shape[1] // local_tokens
    width = first_weight.shape[1]
    bins = distance_weight.shape[1]
    members = 2 * LANES // depth
    groups = block // members
    local_groups = local_tokens // members
    chunks = block // (BATCH * members)

    vmem = pl.BlockSpec(memory_space=pltpu.VMEM)
    hbm = pl.BlockSpec(memory_space=pltpu.HBM)
    pair_out, distogram = pl.pallas_call(
        functools.partial(kernel, ranks, depth, chunks),
        out_shape=(
            pltpu.VMEM(pair_state.shape, jnp.bfloat16),
            pltpu.VMEM((block, block * bins), jnp.bfloat16),
        ),
        in_specs=[hbm] * 17,
        out_specs=(vmem, vmem),
        scratch_shapes=[
            pltpu.VMEM((local_groups, width, members * depth), jnp.bfloat16),
            pltpu.VMEM((local_tokens, width * depth), jnp.bfloat16),
            pltpu.VMEM((groups, width, members * depth), jnp.bfloat16),
            pltpu.VMEM((ranks, local_tokens, width * depth), jnp.bfloat16),
            pltpu.VMEM((BATCH * members * block, width * width), jnp.bfloat16),
            pltpu.VMEM(outer_product_weight.shape, jnp.bfloat16),
            pltpu.VMEM(outer_product_weight.shape, jnp.float32),
            pltpu.VMEM(outer_product_weight.shape, jnp.bfloat16),
            pltpu.VMEM((block * (block + 1), channels), jnp.float32),
            pltpu.VMEM((block, channels), jnp.float32),
            pltpu.VMEM((block, channels), jnp.float32),
            pltpu.VMEM((block // 2, block, 2 * bins), jnp.bfloat16),
            pltpu.VMEM((block // 2, block, 2 * bins), jnp.bfloat16),
            pltpu.VMEM((block // 2, block, 2 * bins), jnp.float32),
            pltpu.VMEM((BATCH * members * block, channels), jnp.float32),
            pltpu.VMEM((BATCH * members * block, channels), jnp.bfloat16),
            pltpu.SemaphoreType.DMA((ranks,)),
            pltpu.SemaphoreType.DMA((ranks,)),
            pltpu.SemaphoreType.DMA((ranks,)),
            pltpu.SemaphoreType.DMA((ranks,)),
            pltpu.SemaphoreType.DMA((2, chunks)),
            pltpu.SemaphoreType.DMA((2, chunks)),
            pltpu.VMEM((chunks, block // 4 // chunks, block, 2 * bins), jnp.bfloat16),
            pltpu.SemaphoreType.DMA((chunks,)),
            pltpu.SemaphoreType.DMA((chunks,)),
            pltpu.VMEM((2 * bins, 2 * channels), jnp.bfloat16),
            pltpu.VMEM((1, 2 * bins), jnp.float32),
            pltpu.VMEM((token_kinds.shape[0], channels), jnp.float32),
            pltpu.VMEM(pair_state.shape, pair_state.dtype),
            pltpu.VMEM((1, token_kinds.shape[0]), jnp.int32),
            pltpu.VMEM(first_type_table.shape, jnp.bfloat16),
            pltpu.VMEM(second_type_table.shape, jnp.bfloat16),
            pltpu.VMEM(alignment_state.shape, jnp.bfloat16),
            pltpu.VMEM((local_tokens, depth), jnp.int32),
            pltpu.VMEM(alignment_table.shape, jnp.bfloat16),
            pltpu.VMEM(first_weight.shape, jnp.bfloat16),
            pltpu.VMEM(second_weight.shape, jnp.bfloat16),
            pltpu.VMEM((1, channels), jnp.bfloat16),
            pltpu.SMEM(pair_block_mask.shape, jnp.int32),
            pltpu.VMEM((1, channels), jnp.float32),
            pltpu.VMEM(transition_gate_up.shape, transition_gate_up.dtype),
            pltpu.VMEM(transition_down.shape, transition_down.dtype),
            pltpu.VMEM((bins, channels), jnp.bfloat16),
            pltpu.VMEM((1, bins), jnp.float32),
            pltpu.SemaphoreType.DMA((17,)),
        ],
        compiler_params=pltpu.CompilerParams(
            collective_id=0,
            has_side_effects=True,
            vmem_limit_bytes=56 * 1024 * 1024,
        ),
    )(
        pair_state,
        token_kinds[None],
        first_type_table,
        second_type_table,
        alignment_state,
        alignment_index.T,
        alignment_table,
        first_weight,
        second_weight,
        outer_product_weight,
        outer_product_bias[None],
        pair_block_mask,
        transition_gain[None],
        transition_gate_up,
        transition_down,
        distance_weight.T,
        distance_bias[None],
    )
    return pl.pallas_call(
        store,
        out_shape=(
            jax.ShapeDtypeStruct(pair_state.shape, jnp.bfloat16),
            jax.ShapeDtypeStruct((block, block * bins), jnp.bfloat16),
        ),
        in_specs=[vmem, vmem],
        out_specs=(hbm, hbm),
        scratch_shapes=[pltpu.SemaphoreType.DMA((2, STORES))],
    )(
        pltpu.with_memory_space_constraint(pair_out, pltpu.VMEM),
        pltpu.with_memory_space_constraint(distogram, pltpu.VMEM),
    )


def solution(mesh):
    in_specs = (
        P(("conf", "row"), "col", None),
        P("conf"),
        P(),
        P(),
        P(None, ("conf", "row", "col")),
        P(None, ("conf", "row", "col")),
        P(),
        P(),
        P(),
        P(),
        P(),
        P(("conf", "row"), "col"),
        P(),
        P(),
        P(),
        P(),
        P(),
    )
    out_specs = (P(("conf", "row"), "col", None), P(("conf", "row"), "col"))
    return jax.shard_map(
        functools.partial(local, mesh.shape["col"]),
        mesh=mesh,
        in_specs=in_specs,
        out_specs=out_specs,
        check_vma=False,
    )
```
